32 devices in a mesh: groups: 2 (over x), blk: 16 (over z, y, core).
Axes of the slice: x: 2, y: 2, z: 4, core: 2. Of those that a mesh axis runs over, the one named last changes fastest.
Arguments:
- points: bfloat16 [49152, 1024], P(('groups', 'blk')), parts along dimension 0, may hold values from -6 to 6
- coverage: float32 [49152], P(('groups', 'blk')), parts along dimension 0, may hold values from 0 to 1.5
- candidates: bfloat16 [4096, 1024], P(('groups', 'blk')), parts along dimension 0, may hold values from -6 to 6
- cand_count: int32 [32], P(('groups', 'blk')), parts along dimension 0, may hold values from 16 to 128, as said below
- acc_index: int32 [32, 16], P(('groups', 'blk')), parts along dimension 0, may hold values from 0 to 127, as said below
Outputs:
- gain_out: float32 [4096], P(('groups', 'blk')), parts along dimension 0
- new_coverage: float32 [49152], P(('groups', 'blk')), parts along dimension 0
The draws below stay inside these ranges and needn't reach their ends.
There are 2 independent parts, one for each index of `groups`. The reference program is written for one: setup_inputs(seed, part) draws one part's arguments, and reference() takes and returns one part's arrays. A program takes and returns all parts, laid end to end along the dimension named above; each array names one. Nothing has to cross between parts.
Inputs may be any that keep to these rules, and one draw needn't show every extreme that they name: `cand_count`: some device has all 128 slots live. `acc_index`: each entry of row b is below cand_count[b]; entries may repeat.
All inputs are finite; a program needn't handle non-finite values.
Results may differ from the reference program's by a relative error of at most 0.0003.
Values may be sent and summed in bfloat16 or wider, within the bound.
No kernel may reach another device: no remote copies, remote signals or barrier semaphores. Data moves between devices by JAX's collectives and lax.ppermute only.
A program may use at most 64 MiB of HBM per device.

```python
import jax
import jax.numpy as jnp
from jax import lax

D = 1024
CAND_DEV = 128
ACC_DEV = 16
PTS = 24576
CANDS = 2048
N_BLK = 16


def shared_counts(key):
    first, second = jax.random.split(jax.random.fold_in(key, 7))
    counts = jax.random.randint(first, (N_BLK,), ACC_DEV, CAND_DEV + 1)
    chosen = jax.random.randint(second, (), 0, N_BLK)
    return jnp.where(jnp.arange(N_BLK) == chosen, CAND_DEV, counts).astype(jnp.int32)


def draw_cand_count(key, part):
    return shared_counts(key)


def draw_acc_index(key, part):
    counts = shared_counts(key)
    picked = jax.random.randint(jax.random.fold_in(key, 11), (N_BLK, ACC_DEV), 0, counts[:, None])
    return picked.astype(jnp.int32)


def levels(stream_key, dims, cuts, least, high):
    def one(axis_at, parts):
        heights = jax.random.uniform(jax.random.fold_in(jax.random.fold_in(stream_key, 6), axis_at), (parts,), jnp.float32, least / len(cuts), high / len(cuts))
        return jnp.repeat(jnp.exp(heights), dims[axis_at] // parts).reshape((-1,) + (1,) * (len(dims) - axis_at - 1))

    loudness = one(*cuts[0])
    for cut in cuts[1:]:
        loudness = loudness * one(*cut)
    return loudness


def noise(key, dims, width, bound, cuts=(), kind=jnp.bfloat16):
    result = jax.random.normal(key, dims, jnp.float32) * width
    if len(cuts) > 0:
        result = levels(key, dims, cuts, -0.22, 0.18) * result
    return jnp.clip(result, min=-bound, max=bound).astype(kind)


def setup_inputs(seed: int = 0, part: int = 0) -> dict:
    arg_keys = jax.random.split(jax.random.key(seed), 6)
    part_splits = jax.random.split(jax.random.fold_in(arg_keys[5], part), 6)
    points = noise(part_splits[0], (PTS, D), 1.0, 6.0, ((0, 16),))
    coverage = jnp.clip(1.5 * jax.random.uniform(part_splits[1], (PTS,), jnp.float32) ** levels(part_splits[1], (PTS,), ((0, 16),), -0.2, 0.2), 0.0, 1.5)
    candidates = noise(part_splits[2], (CANDS, D), 1.0, 6.0, ((0, 16),))
    cand_count = draw_cand_count(jax.random.fold_in(jax.random.fold_in(arg_keys[5], part), 71), part)
    acc_index = draw_acc_index(jax.random.fold_in(jax.random.fold_in(arg_keys[5], part), 71), part)
    return dict(points=points, coverage=coverage, candidates=candidates, cand_count=cand_count, acc_index=acc_index)


def block_gains(points, coverage, cand_block, factor):
    similar = jnp.dot(points, cand_block.T, preferred_element_type=jnp.float32) * factor
    return lax.optimization_barrier(jnp.sum(jnp.maximum(similar - coverage[:, None], 0.0), axis=0))

def reference(points, coverage, candidates, cand_count, acc_index):
    factor = 1.0 / jnp.sqrt(jnp.float32(D))
    blocks = candidates.reshape(N_BLK, CAND_DEV, D)
    gain_sum = lax.map(lambda cand_block: block_gains(points, coverage, cand_block, factor), blocks)
    live_rows = jnp.arange(CAND_DEV, dtype=jnp.int32)[None, :] < cand_count[:, None]
    gain_out = jnp.where(live_rows, gain_sum / jnp.float32(PTS), 0.0).reshape(CANDS)
    rows_taken = (jnp.arange(N_BLK, dtype=jnp.int32)[:, None] * CAND_DEV + acc_index).reshape(-1)
    accepted = jnp.take(candidates, rows_taken, axis=0)
    similar = jnp.dot(points, accepted.T, preferred_element_type=jnp.float32) * factor
    new_coverage = jnp.maximum(coverage, lax.optimization_barrier(jnp.max(similar, axis=1)))
    return (gain_out, new_coverage)
```

```python
import functools
import math

import jax
import jax.numpy as jnp
from jax import lax
from jax.experimental import pallas as pl
from jax.experimental.pallas import tpu as pltpu
from jax.sharding import PartitionSpec as P

F32 = jnp.float32
LANES = 128
SUBLANES = 8
CORES = 2
VMEM_SPEC = pl.BlockSpec(memory_space=pltpu.VMEM)


def chip_ring(mesh):
    row = mesh.devices.reshape(-1, mesh.shape["blk"])[0]
    chips = len(row) // CORES
    natural = list(range(chips))
    coords = [getattr(row[CORES * c], "coords", None) for c in natural]
    if any(c is None for c in coords):
        return natural

    def near(a, b):
        return sum(abs(u - v) for u, v in zip(coords[a], coords[b])) == 1

    def grow(path, left):
        if not left:
            return path if near(path[-1], path[0]) else None
        for c in sorted(left):
            if near(path[-1], c):
                found = grow(path + [c], left - {c})
                if found:
                    return found
        return None

    if chips > 2 and len({c[:2] for c in map(tuple, coords)}) > 1:
        return grow([0], frozenset(natural[1:])) or natural
    return natural


def score_body(tile, blocks, *refs):
    pts, covs, runs = refs[0:2], refs[2:4], refs[4:6]
    cands, biases = refs[6 : 6 + blocks], refs[6 + blocks : 6 + 2 * blocks]
    outs = refs[6 + 2 * blocks :]
    new_runs, sums = outs[0:2], outs[2:]
    block = jnp.concatenate([c[...] for c in cands], axis=0)
    slots = cands[0].shape[0]
    rows = blocks * slots
    bias = jnp.concatenate(
        [jnp.broadcast_to(b[0:1, :], (slots, slots)).T[:, :LANES] for b in biases], axis=0
    )
    wide = jnp.concatenate([bias] * (tile // LANES), axis=1)
    total = jnp.zeros((rows, LANES), F32)
    for half in range(2):
        for at in range(0, pts[half].shape[0], tile):
            span = pl.ds(at, tile)
            dots = lax.dot_general(
                block,
                pts[half][span, :],
                (((1,), (1,)), ((), ())),
                preferred_element_type=F32,
            )
            over = jnp.maximum(dots - covs[half][0:1, span], 0.0)
            for lane in range(0, tile, LANES):
                total = total + over[:, lane : lane + LANES]
            taken = (dots + wide).reshape(rows // SUBLANES, SUBLANES, tile)
            new_runs[half][:, span] = jnp.maximum(runs[half][:, span], jnp.max(taken, axis=0))
    for b in range(blocks):
        part = jnp.sum(total[b * slots : (b + 1) * slots].T, axis=0, keepdims=True)
        sums[b][...] = jnp.broadcast_to(part, (SUBLANES, slots))


def score(pts, covs, runs, cands, biases):
    blocks = len(cands)
    slots, width = cands[0].shape
    points = pts[0].shape[0]
    tile = math.gcd(points, 256)
    run_shape = jax.ShapeDtypeStruct(runs[0].shape, F32)
    out = pl.pallas_call(
        functools.partial(score_body, tile, blocks),
        out_shape=[run_shape] * 2 + [jax.ShapeDtypeStruct((SUBLANES, slots), F32)] * blocks,
        in_specs=[VMEM_SPEC] * (6 + 2 * blocks),
        out_specs=[VMEM_SPEC] * (2 + blocks),
        input_output_aliases={4: 0, 5: 1},
        compiler_params=pltpu.CompilerParams(vmem_limit_bytes=16 << 20),
        cost_estimate=pl.CostEstimate(
            flops=2 * blocks * slots * 2 * points * width,
            bytes_accessed=2 * points * width * 2,
            transcendentals=0,
        ),
    )(*pts, *covs, *runs, *cands, *biases)
    return out[0:2], out[2:]


def per_device(ring, points, coverage, candidates, cand_count, acc_index):
    width = points.shape[1]
    slots = candidates.shape[0]
    chips = len(ring)
    devices = chips * CORES
    root = math.sqrt(width)
    at = {c: p for p, c in enumerate(ring)}

    def pairs(shift):
        found = []
        for i in range(devices):
            chip, core = divmod(i, CORES)
            to = ring[(at[chip] + (shift if core == 0 else -shift)) % chips]
            found.append((i, to * CORES + core))
        return found

    def move(x, shift):
        return lax.ppermute(x, "blk", pairs(shift))

    swap = [(i, i ^ 1) for i in range(devices)]
    slot_ids = jnp.arange(slots, dtype=jnp.int32)
    marked = jnp.any(acc_index[0][:, None] == slot_ids[None, :], axis=0)
    bias = jnp.broadcast_to(jnp.where(marked, 0.0, -jnp.inf), (SUBLANES, slots)).astype(F32)
    cov = (coverage * root)[None, :]

    got = {}
    offset = {}
    for k in range(1, chips):
        step = 1 if k % 2 else -1
        source = (candidates, bias) if k <= 2 else got[k - 2]
        got[k] = (move(source[0], step), move(source[1], step))
        offset[k] = step * ((k + 1) // 2)
    pts = (points, lax.ppermute(points, "blk", swap))
    covs = (cov, lax.ppermute(cov, "blk", swap))
    low = jnp.full((SUBLANES, points.shape[0]), -jnp.inf, F32)
    runs = (low, low)
    runs, sums = score(pts, covs, runs, [candidates], [bias])
    gain = sums[0][0]
    order = list(range(1, chips))
    for first in range(0, len(order), 2):
        ks = order[first : first + 2]
        runs, sums = score(pts, covs, runs, [got[k][0] for k in ks], [got[k][1] for k in ks])
        for k, s in zip(ks, sums):
            gain = gain + move(s[0:1], -offset[k])[0]
    other = lax.ppermute(jnp.max(runs[1], axis=0), "blk", swap)
    best = jnp.maximum(jnp.max(runs[0], axis=0), other)
    new_coverage = jnp.maximum(coverage, best / root)
    live = slot_ids < cand_count[0]
    total = F32(points.shape[0] * devices) * root
    return jnp.where(live, gain / total, 0.0), new_coverage


def solution(mesh):
    split = P(("groups", "blk"))
    wide = P(("groups", "blk"), None)
    return jax.shard_map(
        functools.partial(per_device, chip_ring(mesh)),
        mesh=mesh,
        in_specs=(wide, split, wide, split, wide),
        out_specs=(split, split),
        check_vma=False,
    )
```

```python
import functools
import math

import jax
import jax.numpy as jnp
from jax import lax
from jax.experimental import pallas as pl
from jax.experimental.pallas import tpu as pltpu
from jax.sharding import PartitionSpec as P


F32 = jnp.float32
LANES = 128
SUBLANES = 8
CORES = 2
VMEM_SPEC = pl.BlockSpec(memory_space=pltpu.VMEM)


def chip_ring(mesh):
    row = mesh.devices.reshape(-1, mesh.shape["blk"])[0]
    natural = list(range(len(row) // CORES))
    coords = [getattr(row[CORES * c], "coords", None) for c in natural]
    if any(c is None for c in coords) or len({tuple(c)[:2] for c in coords}) == 1:
        return natural

    def near(a, b):
        return sum(abs(u - v) for u, v in zip(coords[a], coords[b])) == 1

    def grow(path, left):
        if not left:
            return path if near(path[-1], path[0]) else None
        for c in sorted(left):
            if near(path[-1], c):
                found = grow(path + [c], left - {c})
                if found:
                    return found
        return None

    return grow([0], frozenset(natural[1:])) or natural


def score_body(tile, halves, blocks, carried, *refs):
    refs = list(refs)

    def take(n):
        out, refs[:n] = refs[:n], []
        return out

    pts, covs, runs = take(halves), take(halves), take(halves)
    cands, biases, before = take(blocks), take(blocks), take(carried)
    new_runs, (out,) = take(halves), take(1)
    block = jnp.concatenate([c[...] for c in cands], axis=0)
    slots = cands[0].shape[0]
    rows = blocks * slots
    bias = jnp.concatenate(
        [jnp.broadcast_to(b[0:1, :], (slots, slots)).T[:, :LANES] for b in biases], axis=0
    )
    wide = jnp.concatenate([bias] * (tile // LANES), axis=1)
    total = before[0][...] if carried else jnp.zeros((rows, LANES), F32)
    for half in range(halves):
        for at in range(0, pts[half].shape[0], tile):
            span = pl.ds(at, tile)
            dots = lax.dot_general(
                block,
                pts[half][span, :],
                (((1,), (1,)), ((), ())),
                preferred_element_type=F32,
            )
            over = jnp.maximum(dots - covs[half][0:1, span], 0.0)
            for lane in range(0, tile, LANES):
                total = total + over[:, lane : lane + LANES]
            taken = (dots + wide).reshape(rows // SUBLANES, SUBLANES, tile)
            new_runs[half][:, span] = jnp.maximum(runs[half][:, span], jnp.max(taken, axis=0))
    if out.shape[0] == rows:
        out[...] = total
    else:
        for b in range(blocks):
            part = total[b * slots : (b + 1) * slots]
            out[b : b + 1, :] = jnp.sum(part.T, axis=0, keepdims=True)


def score(pts, covs, runs, cands, biases, before=None, last=True):
    halves, blocks = len(pts), len(cands)
    slots, width = cands[0].shape
    points = pts[0].shape[0]
    tile = math.gcd(points, 256)
    carried = () if before is None else (before,)
    out_rows = blocks if last else blocks * slots
    out = pl.pallas_call(
        functools.partial(score_body, tile, halves, blocks, len(carried)),
        out_shape=[jax.ShapeDtypeStruct(r.shape, F32) for r in runs]
        + [jax.ShapeDtypeStruct((out_rows, slots if last else LANES), F32)],
        in_specs=[VMEM_SPEC] * (3 * halves + 2 * blocks + len(carried)),
        out_specs=[VMEM_SPEC] * (halves + 1),
        input_output_aliases={2 * halves + h: h for h in range(halves)},
        compiler_params=pltpu.CompilerParams(vmem_limit_bytes=16 << 20),
        cost_estimate=pl.CostEstimate(
            flops=2 * blocks * slots * halves * points * width,
            bytes_accessed=halves * points * width * 2,
            transcendentals=0,
        ),
    )(*pts, *covs, *runs, *cands, *biases, *carried)
    return list(out[:halves]), out[halves]


def per_device(ring, points, coverage, candidates, cand_count, acc_index):
    width = points.shape[1]
    slots = candidates.shape[0]
    chips = len(ring)
    devices = chips * CORES
    root = math.sqrt(width)
    at = {c: p for p, c in enumerate(ring)}

    def move(x, step, cross):
        pairs = []
        for i in range(devices):
            chip, core = divmod(i, CORES)
            to = ring[(at[chip] + (step if core == 0 else -step)) % chips]
            pairs.append((i, to * CORES + (core ^ cross)))
        return lax.ppermute(x, "blk", pairs)

    def swap(x):
        return move(x, 0, 1)

    slot_ids = jnp.arange(slots, dtype=jnp.int32)
    marked = jnp.any(acc_index[0][:, None] == slot_ids[None, :], axis=0)
    bias = jnp.broadcast_to(jnp.where(marked, 0.0, -jnp.inf), (SUBLANES, slots)).astype(F32)
    cov = (coverage * root)[None, :]

    pts = [points, swap(points)]
    covs = [cov, swap(cov)]
    low = jnp.full((SUBLANES, points.shape[0]), -jnp.inf, F32)
    blocks, offsets = {}, {}
    for k in range(1, chips):
        hop = (k + 1) // 2
        step = (1 if k % 2 else -1) * (1 if hop % 2 else -1)
        source = (candidates, bias) if k <= 2 else blocks[k - 2]
        blocks[k] = (move(source[0], step, 1), move(source[1], step, 1))
        offsets[k] = (step * hop) % chips
    run_a, total = score(pts[:1], covs[:1], [low], [candidates], [bias], last=False)
    run_b, own = score(pts[1:], covs[1:], [low], [candidates], [bias], before=total)
    runs = run_a + run_b
    parts = {0: own}
    for k in range(2, chips + 1, 2):
        ks = [j for j in (k - 1, k) if j < chips]
        runs, sums = score(pts, covs, runs, [blocks[j][0] for j in ks], [blocks[j][1] for j in ks])
        for row, j in enumerate(ks):
            parts[offsets[j]] = sums[row : row + 1]
    h = 1
    while h < chips:
        cross = 1 if h == 1 else 0
        send = [e for e in sorted(parts) if e % (2 * h) == h]
        came = move(jnp.concatenate([parts.pop(e) for e in send], axis=0), h, cross)
        for row, e in enumerate(send):
            to = (1 - e if cross else e - h) % chips
            parts[to] = parts[to] + came[row : row + 1]
        h *= 2
    other = swap(jnp.max(runs[1], axis=0))
    best = jnp.maximum(jnp.max(runs[0], axis=0), other)
    new_coverage = jnp.maximum(coverage, best / root)
    live = slot_ids < cand_count[0]
    total = F32(points.shape[0] * devices) * root
    return jnp.where(live, parts[0][0] / total, 0.0), new_coverage


def solution(mesh):
    split = P(("groups", "blk"))
    wide = P(("groups", "blk"), None)
    ring = chip_ring(mesh)

    def body(*args):
        return per_device(ring, *args)

    return jax.shard_map(
        body,
        mesh=mesh,
        in_specs=(wide, split, wide, split, wide),
        out_specs=(split, split),
        check_vma=False,
    )
```

```python
import functools
import math

import jax
import jax.numpy as jnp
from jax import lax
from jax.experimental import pallas as pl
from jax.experimental.pallas import tpu as pltpu
from jax.sharding import PartitionSpec as P


F32 = jnp.float32
LANES = 128
SUBLANES = 8
CORES = 2
VMEM_SPEC = pl.BlockSpec(memory_space=pltpu.VMEM)


def chip_ring(mesh):
    row = mesh.devices.reshape(-1, mesh.shape["blk"])[0]
    natural = list(range(len(row) // CORES))
    coords = [getattr(row[CORES * c], "coords", None) for c in natural]
    if any(c is None for c in coords) or len({tuple(c)[:2] for c in coords}) == 1:
        return natural

    def near(a, b):
        return sum(abs(u - v) for u, v in zip(coords[a], coords[b])) == 1

    def grow(path, left):
        if not left:
            return path if near(path[-1], path[0]) else None
        for c in sorted(left):
            if near(path[-1], c):
                found = grow(path + [c], left - {c})
                if found:
                    return found
        return None

    return grow([0], frozenset(natural[1:])) or natural


def bias_column(picks, slots):
    slot = lax.broadcasted_iota(jnp.int32, (slots, picks.shape[1]), 0)
    hit = jnp.where(slot == picks, 0.0, -jnp.inf)
    return jnp.max(hit, axis=1, keepdims=True)


def scan_points(block, bias, tiles, total):
    rows = block.shape[0]
    for load, cov, keep, store in tiles:
        dots = lax.dot_general(
            block, load(), (((1,), (1,)), ((), ())), preferred_element_type=F32
        )
        tile = dots.shape[1]
        over = jnp.maximum(dots - cov(), 0.0)
        for lane in range(0, tile, LANES):
            total = total + over[:, lane : lane + LANES]
        best = jnp.max((dots + bias).reshape(rows // SUBLANES, SUBLANES, tile), axis=0)
        store(best if keep is None else jnp.maximum(keep(), best))
    return total


def finish(total, slots, out):
    if out.shape[0] == total.shape[0]:
        out[...] = total
    else:
        for b in range(total.shape[0] // slots):
            part = total[b * slots : (b + 1) * slots]
            out[b : b + 1, :] = jnp.sum(part.T, axis=0, keepdims=True)


def tile_of(points):
    return math.gcd(points, 256)


def scale_body(root, cov, out):
    out[...] = cov[...] * root


def scaled(root, coverage, slack):
    return pl.pallas_call(
        functools.partial(scale_body, root),
        out_shape=jax.ShapeDtypeStruct((1, coverage.shape[0]), F32),
        in_specs=[VMEM_SPEC],
        out_specs=VMEM_SPEC,
        compiler_params=pltpu.CompilerParams(vmem_limit_bytes=4 << 20),
        cost_estimate=pl.CostEstimate(flops=slack, bytes_accessed=0, transcendentals=0),
    )(coverage[None, :])


def score_body(halves, blocks, fresh, carried, *refs):
    refs = list(refs)

    def take(n):
        got, refs[:n] = refs[:n], []
        return got

    pts, covs, runs = take(halves), take(halves), take(0 if fresh else halves)
    cands, picks, before = take(blocks), take(blocks), take(carried)
    new_runs, (out,) = take(halves), take(1)
    block = jnp.concatenate([c[...] for c in cands], axis=0)
    slots = cands[0].shape[0]
    bias = jnp.concatenate([bias_column(p[...], slots) for p in picks], axis=0)
    total = before[0][...] if carried else jnp.zeros((blocks * slots, LANES), F32)

    def keep(half, span):
        return runs[half][:, span]

    def store(half, span, x):
        new_runs[half][:, span] = x

    tiles = []
    for half in range(halves):
        tile = tile_of(pts[half].shape[0])
        for at in range(0, pts[half].shape[0], tile):
            span = pl.ds(at, tile)
            tiles.append(
                (
                    lambda half=half, span=span: pts[half][span, :],
                    lambda half=half, span=span: covs[half][0:1, span],
                    None if fresh else functools.partial(keep, half, span),
                    functools.partial(store, half, span),
                )
            )
    finish(scan_points(block, bias, tiles, total), slots, out)


def score(pts, covs, runs, cands, picks, before=None, last=True):
    halves, blocks = len(pts), len(cands)
    slots, width = cands[0].shape
    points = pts[0].shape[0]
    fresh = runs is None
    carried = () if before is None else (before,)
    run_shape = jax.ShapeDtypeStruct((SUBLANES, points), F32)
    out_shape = (blocks, slots) if last else (blocks * slots, LANES)
    kept = [] if fresh else runs
    out = pl.pallas_call(
        functools.partial(score_body, halves, blocks, fresh, len(carried)),
        out_shape=[run_shape] * halves + [jax.ShapeDtypeStruct(out_shape, F32)],
        in_specs=[VMEM_SPEC] * (2 * halves + len(kept) + 2 * blocks + len(carried)),
        out_specs=[VMEM_SPEC] * (halves + 1),
        input_output_aliases={} if fresh else {2 * halves + h: h for h in range(halves)},
        compiler_params=pltpu.CompilerParams(vmem_limit_bytes=16 << 20),
        cost_estimate=pl.CostEstimate(
            flops=2 * blocks * slots * halves * points * width,
            bytes_accessed=halves * points * width * 2,
            transcendentals=0,
        ),
    )(*pts, *covs, *kept, *cands, *picks, *carried)
    return list(out[:halves]), out[halves]


def per_device(ring, points, coverage, candidates, cand_count, acc_index):
    width = points.shape[1]
    slots = candidates.shape[0]
    chips = len(ring)
    devices = chips * CORES
    root = math.sqrt(width)
    at = {c: p for p, c in enumerate(ring)}

    def move(x, step, cross):
        pairs = []
        for i in range(devices):
            chip, core = divmod(i, CORES)
            to = ring[(at[chip] + (step if core == 0 else -step)) % chips]
            pairs.append((i, to * CORES + (core ^ cross)))
        return lax.ppermute(x, "blk", pairs)

    def swap(x):
        return move(x, 0, 1)

    cov = scaled(root, coverage, 32 * slots * points.shape[0] * width)
    pts = [points, swap(points)]
    covs = [cov, swap(cov)]
    alone = [candidates], [acc_index]
    run_a, total = score(pts[:1], covs[:1], None, *alone, last=False)
    run_b, gain = score(pts[1:], covs[1:], None, *alone, before=total)
    runs = run_a + run_b

    blocks, picks, parts, home = {}, {}, {}, {}
    for k in range(1, chips):
        hop = (k + 1) // 2
        step = (1 if k % 2 else -1) * (1 if hop % 2 else -1)
        home[k] = (step * hop) % chips
        blocks[k] = move(candidates if k <= 2 else blocks[k - 2], step, 1)
        picks[k] = move(acc_index if k <= 2 else picks[k - 2], step, 1)
    for k in range(2, chips + 1, 2):
        ks = [j for j in (k - 1, k) if j < chips]
        group = [blocks[j] for j in ks], [picks[j] for j in ks]
        if k < chips - 2:
            run_a, total = score(pts[:1], covs[:1], runs[:1], *group, last=False)
            run_b, sums = score(pts[1:], covs[1:], runs[1:], *group, before=total)
            runs = run_a + run_b
        else:
            runs, sums = score(pts, covs, runs, *group)
        parts.update({home[j]: sums[row : row + 1] for row, j in enumerate(ks)})
    odd = [e for e in sorted(parts) if e % 2]
    came = move(jnp.concatenate([parts[e] for e in odd], axis=0), 1, 1)
    for row, e in enumerate(odd):
        to = (1 - e) % chips
        if to:
            parts[to] = parts[to] + came[row : row + 1]
        else:
            gain = gain + came[row : row + 1]
    for e in sorted(parts):
        if e and e % 2 == 0:
            gain = gain + move(parts[e], e, 0)
    other = swap(jnp.max(runs[1], axis=0))
    best = jnp.maximum(jnp.max(runs[0], axis=0), other)
    new_coverage = jnp.maximum(coverage, best / root)
    live = jnp.arange(slots, dtype=jnp.int32) < cand_count[0]
    scale = F32(points.shape[0] * devices) * root
    return jnp.where(live, gain[0] / scale, 0.0), new_coverage


def solution(mesh):
    split = P(("groups", "blk"))
    wide = P(("groups", "blk"), None)
    ring = chip_ring(mesh)

    def body(*args):
        return per_device(ring, *args)

    return jax.shard_map(
        body,
        mesh=mesh,
        in_specs=(wide, split, wide, split, wide),
        out_specs=(split, split),
        check_vma=False,
    )
```

```python
import functools
import math

import jax
import jax.numpy as jnp
from jax import lax
from jax.experimental import pallas as pl
from jax.experimental.pallas import tpu as pltpu
from jax.sharding import PartitionSpec as P


F32 = jnp.float32
LANES = 128
SUBLANES = 8
CORES = 2
VMEM_SPEC = pl.BlockSpec(memory_space=pltpu.VMEM)


def chip_ring(mesh):
    row = mesh.devices.reshape(-1, mesh.shape["blk"])[0]
    natural = list(range(len(row) // CORES))
    coords = [getattr(row[CORES * c], "coords", None) for c in natural]
    if any(c is None for c in coords) or len({tuple(c)[:2] for c in coords}) == 1:
        return natural

    def near(a, b):
        return sum(abs(u - v) for u, v in zip(coords[a], coords[b])) == 1

    def grow(path, left):
        if not left:
            return path if near(path[-1], path[0]) else None
        for c in sorted(left):
            if near(path[-1], c):
                found = grow(path + [c], left - {c})
                if found:
                    return found
        return None

    return grow([0], frozenset(natural[1:])) or natural


def bias_column(picks, slots):
    slot = lax.broadcasted_iota(jnp.int32, (slots, picks.shape[1]), 0)
    hit = jnp.where(slot == picks[0:1].astype(jnp.int32), 0.0, -jnp.inf)
    return jnp.max(hit, axis=1, keepdims=True)


def scan_points(block, bias, tiles, total):
    rows = block.shape[0]
    for load, cov, keep, store in tiles:
        dots = lax.dot_general(
            block, load(), (((1,), (1,)), ((), ())), preferred_element_type=F32
        )
        tile = dots.shape[1]
        over = jnp.maximum(dots - cov(), 0.0)
        for lane in range(0, tile, LANES):
            total = total + over[:, lane : lane + LANES]
        best = jnp.max((dots + bias).reshape(rows // SUBLANES, SUBLANES, tile), axis=0)
        store(best if keep is None else jnp.maximum(keep(), best))
    return total


def finish(total, slots, out):
    if out.shape[0] == total.shape[0]:
        out[...] = total
    else:
        for b in range(total.shape[0] // slots):
            part = total[b * slots : (b + 1) * slots]
            out[b : b + 1, :] = jnp.sum(part.T, axis=0, keepdims=True)


def tile_of(points):
    return math.gcd(points, 768)


def scale_body(root, cov, out):
    out[...] = cov[...] * root


def scaled(root, coverage, slack):
    return pl.pallas_call(
        functools.partial(scale_body, root),
        out_shape=jax.ShapeDtypeStruct((1, coverage.shape[0]), F32),
        in_specs=[VMEM_SPEC],
        out_specs=VMEM_SPEC,
        compiler_params=pltpu.CompilerParams(vmem_limit_bytes=4 << 20),
        cost_estimate=pl.CostEstimate(flops=slack, bytes_accessed=0, transcendentals=0),
    )(coverage[None, :])


def score_body(halves, blocks, fresh, carried, *refs):
    refs = list(refs)

    def take(n):
        got, refs[:n] = refs[:n], []
        return got

    pts, covs, runs = take(halves), take(halves), take(0 if fresh else halves)
    cands, picks, before = take(blocks), take(blocks), take(carried)
    new_runs, (out,) = take(halves), take(1)
    block = jnp.concatenate([c[...] for c in cands], axis=0)
    slots = cands[0].shape[0]
    bias = jnp.concatenate([bias_column(p[...], slots) for p in picks], axis=0)
    total = before[0][...] if carried else jnp.zeros((blocks * slots, LANES), F32)

    def keep(half, span):
        return runs[half][:, span]

    def store(half, span, x):
        new_runs[half][:, span] = x

    tiles = []
    for half in range(halves):
        tile = tile_of(pts[half].shape[0])
        for at in range(0, pts[half].shape[0], tile):
            span = pl.ds(at, tile)
            tiles.append(
                (
                    lambda half=half, span=span: pts[half][span, :],
                    lambda half=half, span=span: covs[half][0:1, span],
                    None if fresh else functools.partial(keep, half, span),
                    functools.partial(store, half, span),
                )
            )
    finish(scan_points(block, bias, tiles, total), slots, out)


def score(pts, covs, runs, cands, picks, before=None, last=True):
    halves, blocks = len(pts), len(cands)
    slots, width = cands[0].shape
    points = pts[0].shape[0]
    fresh = runs is None
    carried = () if before is None else (before,)
    run_shape = jax.ShapeDtypeStruct((SUBLANES, points), F32)
    out_shape = (blocks, slots) if last else (blocks * slots, LANES)
    kept = [] if fresh else runs
    out = pl.pallas_call(
        functools.partial(score_body, halves, blocks, fresh, len(carried)),
        out_shape=[run_shape] * halves + [jax.ShapeDtypeStruct(out_shape, F32)],
        in_specs=[VMEM_SPEC] * (2 * halves + len(kept) + 2 * blocks + len(carried)),
        out_specs=[VMEM_SPEC] * (halves + 1),
        input_output_aliases={} if fresh else {2 * halves + h: h for h in range(halves)},
        compiler_params=pltpu.CompilerParams(vmem_limit_bytes=16 << 20),
        cost_estimate=pl.CostEstimate(
            flops=2 * blocks * slots * halves * points * width,
            bytes_accessed=halves * points * width * 2,
            transcendentals=0,
        ),
    )(*pts, *covs, *kept, *cands, *picks, *carried)
    return list(out[:halves]), out[halves]


def rider(chips, j):
    return 6 if j == 0 and chips == 8 else None


def per_device(ring, points, coverage, candidates, cand_count, acc_index):
    width = points.shape[1]
    slots = candidates.shape[0]
    chips = len(ring)
    devices = chips * CORES
    root = math.sqrt(width)
    at = {c: p for p, c in enumerate(ring)}

    def move(x, step, cross):
        pairs = []
        for i in range(devices):
            chip, core = divmod(i, CORES)
            to = ring[(at[chip] + (step if core == 0 else -step)) % chips]
            pairs.append((i, to * CORES + (core ^ cross)))
        return lax.ppermute(x, "blk", pairs)

    def swap(x):
        return move(x, 0, 1)

    cov = scaled(root, coverage, 32 * slots * points.shape[0] * width)
    pts = [points, swap(points)]
    covs = [cov, swap(cov)]

    half = chips // 2

    def step_of(k):
        return (1 if k % 2 else -1) * sign((k + 1) // 2)

    def sign(hop):
        return 1 if hop % 2 else -1

    def row_of(tag):
        return jnp.pad(
            tag[0:1].astype(F32), ((0, 0), (0, slots - tag.shape[1])), constant_values=-1.0
        )

    blocks, tags = {0: candidates}, {0: acc_index}
    for k in range(1, chips):
        blocks[k] = move(blocks[max(k - 2, 0)], step_of(k), 1)
    riders = {rider(chips, j): j for j in range(half - 1)}
    for k in range(1, chips):
        if k not in riders:
            tags[k] = move(tags[max(k - 2, 0)], step_of(k), 1)
    runs = None
    seen = {}
    for j in range(half):
        ks = [2 * j, 2 * j + 1]
        group = [blocks[k] for k in ks], [tags[k] for k in ks]
        if j < half - 2:
            near, far = (None, None) if runs is None else (runs[:1], runs[1:])
            run_a, total = score(pts[:1], covs[:1], near, *group, last=False)
            run_b, sums = score(pts[1:], covs[1:], far, *group, before=total)
            runs = run_a + run_b
        else:
            runs, sums = score(pts, covs, runs, *group)
        if j == 0:
            gain, rows = sums[0:1], [sums[1:2]]
        else:
            rows = [sums[1:2] + seen[j - 1][-1], sums[0:1]]
            if j > 1:
                rows[1] = rows[1] + seen[j - 1][-2]
            rows.reverse()
        if j < half - 1:
            k = rider(chips, j)
            lead = []
            if k is not None:
                tag, rows[0] = lax.optimization_barrier((tags[k - 2], rows[0]))
                lead = [row_of(tag)]
            came = move(jnp.concatenate(lead + rows, axis=0), sign(j + 2), 1)
            if k is not None:
                tags[k] = came
            seen[j] = [came[r : r + 1] for r in range(came.shape[0])]
    gain = gain + move(rows[1], half, half % 2)
    gain = gain + move(rows[0], step_of(chips - 2) * (half - 1), (half - 1) % 2)
    other = swap(jnp.max(runs[1], axis=0))
    best = jnp.maximum(jnp.max(runs[0], axis=0), other)
    new_coverage = jnp.maximum(coverage, best / root)
    live = jnp.arange(slots, dtype=jnp.int32) < cand_count[0]
    scale = F32(points.shape[0] * devices) * root
    return jnp.where(live, gain[0] / scale, 0.0), new_coverage


def solution(mesh):
    split = P(("groups", "blk"))
    wide = P(("groups", "blk"), None)
    ring = chip_ring(mesh)

    def body(*args):
        return per_device(ring, *args)

    return jax.shard_map(
        body,
        mesh=mesh,
        in_specs=(wide, split, wide, split, wide),
        out_specs=(split, split),
        check_vma=False,
    )
```
